32 devices in a mesh: depth: 4 (over z), tx: 2 (over x), ty: 4 (over y, core).
Axes of the slice: x: 2, y: 2, z: 4, core: 2. Of those that a mesh axis runs over, the one named last changes fastest.
Arguments:
- slices: float32 [4, 2, 512, 1024], P('depth', None, 'tx', 'ty'), may hold values from -1.15 to 1.15
- thickness: float32 [4], P('depth'), may hold values from 0.1 to 0.6
- probes: float32 [8, 2, 128, 128], replicated, may hold values from -4 to 4
- centers: int32 [2, 4, 12, 2], P('tx', 'ty'), may hold values from 0 to 255
- batch_of: int32 [2, 4, 12, 1], P('tx', 'ty'), may hold values from 0 to 7; in each aligned block of 12 rows (0 to 11, 12 to 23, ..., all dimensions but the last counted through in order) at most 2 rows name the same one
- intensity: float32 [2, 4, 12, 128, 128], P('tx', 'ty'), may hold values from 0 to 2
Outputs:
- gradient: float32 [4, 2, 512, 1024], P('depth', None, 'tx', 'ty')
The draws below stay inside these ranges and needn't reach their ends.
Inputs may be any that keep to these rules, and one draw needn't show every extreme that they name: `batch_of`: among the windows of one tile, no micro-batch appears more than 2 times.
All inputs are finite; a program needn't handle non-finite values.
Results may differ from the reference program's by a relative error of at most 0.0003.
Values sent between devices are 32-bit elements; how exact they have to be, the bound alone decides.
No kernel may reach another device: no remote copies, remote signals or barrier semaphores. Data moves between devices by JAX's collectives and lax.ppermute only.
A program may use at most 64 MiB of HBM per device.

```python
import math
import jax
import jax.numpy as jnp
import numpy as np
from jax import lax

WINDOW = 128
HALF = 64
TILE = 256
MB = 8
CAP = 2
WIN = 12
SLICES = 4
NX = 512
NY = 1024
N_TX = 2
N_TY = 4


def draw_slices(key, part):
    first_key, second_key = jax.random.split(jax.random.fold_in(key, 11))
    shape = (SLICES, NX, NY)
    magnitude = jax.random.uniform(first_key, shape, jnp.float32, 0.9, 1.1)
    phases = jax.random.uniform(second_key, shape, jnp.float32, -0.6, 0.6)
    return jnp.stack([magnitude * jnp.cos(phases), magnitude * jnp.sin(phases)], axis=1)


def touch_ends(drawn, stream_key, low, largest):
    spot = [jax.random.randint(jax.random.fold_in(stream_key, axis), (), 0, length) for axis, length in enumerate(drawn.shape)]
    longest = drawn.shape.index(max(drawn.shape))
    next_to = spot[:longest] + [(spot[longest] + 1) % drawn.shape[longest]] + spot[longest + 1:]
    return drawn.at[tuple(spot)].set(low).at[tuple(next_to)].set(largest)


def block_levels(rng, shape, pieces, least, largest):
    def one(position, shards_of):
        heights = jax.random.uniform(jax.random.fold_in(jax.random.fold_in(rng, 6), position), (shards_of,), jnp.float32, least / len(pieces), largest / len(pieces))
        return jnp.repeat(jnp.exp(heights), shape[position] // shards_of).reshape((-1,) + (1,) * (len(shape) - position - 1))

    loudness = one(*pieces[0])
    for cut in pieces[1:]:
        loudness = loudness * one(*cut)
    return loudness


def shared_out(own_key, own, number, rows, number_of, top, bound, slope):
    sequence = jax.random.permutation(own_key, number_of)
    crowded, ordinary = load_shares(number_of, rows * top, bound, slope, True), load_shares(number_of, rows * top, bound, slope, False)
    places = jnp.arange(number_of)

    def named(sizes, turn):
        used = int((sizes > 0).sum())
        fixed = max(1, used // 4)
        moved = fixed + (places - fixed + turn * (used - fixed)) % max(1, number_of - fixed)
        return jnp.zeros((number_of,), jnp.int32).at[sequence[jnp.where(places < fixed, places, moved)]].set(jnp.asarray(sizes, jnp.int32))

    sizes = jnp.where(number % 4 == 0, named(crowded, number // 4), named(ordinary, number - number // 4 - 1))
    mixed = jax.random.permutation(jax.random.fold_in(own, 3), number_of)
    donor, taker = mixed[0:number_of // 2 * 2:2], mixed[1:number_of // 2 * 2:2]
    margin = jnp.minimum(sizes[donor] - 1, bound - sizes[taker]) // 2
    margin = jnp.where((donor == sequence[0]) | (taker == sequence[0]) | (sizes[taker] == 0), 0, jnp.maximum(margin, 0))
    moved = jax.random.randint(jax.random.fold_in(own, 4), (number_of // 2,), 0, 1 << 20) % (margin + 1)
    sizes = sizes.at[donor].add(-moved).at[taker].add(moved)
    labels = jnp.searchsorted(jnp.cumsum(sizes), jnp.arange(rows * top), side="right").astype(jnp.int32)
    listing = labels.reshape(top, rows).T
    listing = listing[jax.random.permutation(jax.random.fold_in(own, 1), rows)]
    turn = jax.random.randint(jax.random.fold_in(own, 2), (rows, 1), 0, top)
    return jnp.take_along_axis(listing, (jnp.arange(top)[None, :] + turn) % top, axis=1)


def load_shares(number_of, total, limit, lean, full):
    loads = [(1 << 20) // math.isqrt(grade ** lean) + 1 for grade in range(1, number_of + 1)]
    largest = limit if full else min(limit, max(-(-total // number_of), total * loads[0] // sum(loads)))
    least = 1 if total - largest >= number_of - 1 else 0
    holding, rest = [largest] + [least] * (number_of - 1), total - largest - least * (number_of - 1)
    while rest > 0:
        free = [i for i in range(1, number_of) if holding[i] < largest] or [i for i in range(1, number_of) if holding[i] < limit]
        whole, left = sum([loads[i] for i in free]), rest
        for i in free:
            more = min(limit - holding[i], max(1, left * loads[i] // whole), rest)
            holding[i] = holding[i] + more
            rest = rest - more
    return np.array(holding)


def normal_values(key, dims, spread, reach, held_as=jnp.bfloat16):
    entries = spread * jax.random.normal(key, dims, jnp.float32)
    return jnp.clip(entries, min=-reach, max=reach).astype(held_as)


def setup_inputs(seed: int = 0) -> dict:
    seeds = jax.random.split(jax.random.key(seed), 7)
    slices = draw_slices(jax.random.fold_in(seeds[6], 71), 0)
    thickness = jnp.clip(jnp.exp(math.log(0.6) - 1.7917595 * jax.random.uniform(seeds[1], (SLICES,), jnp.float32) ** block_levels(seeds[1], (SLICES,), ((0, 4),), -0.2, 0.2)), 0.1, 0.6)
    probes = normal_values(seeds[2], (MB, 2, WINDOW, WINDOW), 0.7, 4.0, jnp.float32)
    centers = touch_ends(jax.random.randint(seeds[3], (N_TX, N_TY, WIN, 2), 0, TILE), jax.random.fold_in(seeds[3], 1), 0, TILE - 1).astype(jnp.int32)
    batch_of_keys = jax.random.split(jax.random.fold_in(seeds[4], 1), N_TX * N_TY * WIN // WIN)
    batch_of_turns = jax.random.permutation(jax.random.fold_in(seeds[4], 3), N_TX * N_TY * WIN // WIN)
    batch_of = jax.vmap(lambda own, number: shared_out(jax.random.fold_in(seeds[4], 2), own, number, WIN, MB, 1, CAP, 2))(batch_of_keys, batch_of_turns).reshape((N_TX, N_TY, WIN, 1))
    intensity = jnp.clip(2.0 * jax.random.uniform(seeds[5], (N_TX, N_TY, WIN, WINDOW, WINDOW), jnp.float32) ** block_levels(seeds[5], (N_TX, N_TY, WIN, WINDOW, WINDOW), ((0, 2), (1, 4)), -0.2, 0.2), 0.0, 2.0)
    return {"slices": slices, "thickness": thickness, "probes": probes, "centers": centers, "batch_of": batch_of, "intensity": intensity}


def kernel_planes(thick):
    counts = jnp.arange(WINDOW, dtype=jnp.int32)
    offset = (counts + HALF) % WINDOW - HALF
    squares = offset[:, None] * offset[:, None] + offset[None, :] * offset[None, :]
    phases = thick * (squares.astype(jnp.float32) * (math.pi / (HALF * HALF)))
    return jnp.cos(phases), jnp.sin(phases)


def transform(values):
    return jnp.fft.fft2(values, norm="ortho")


def inverse(values):
    return jnp.fft.ifft2(values, norm="ortho")


def window_terms(illumination, patches, kernels, target):
    def forward(carried, inputs):
        patch_now, kernel_now = inputs
        incident = inverse(kernel_now * transform(carried))
        return incident * patch_now, incident

    leaving, incidents = lax.scan(forward, illumination, (patches, kernels))
    detector = transform(leaving)
    residue = 2.0 * (jnp.real(detector) ** 2 + jnp.imag(detector) ** 2 - target) * detector

    def backward(returning, inputs):
        patch_now, kernel_now, incident = inputs
        slice_term = jnp.conj(incident) * returning
        returning = inverse(jnp.conj(kernel_now) * transform(jnp.conj(patch_now) * returning))
        return returning, slice_term

    _, slice_terms = lax.scan(backward, inverse(residue), (patches, kernels, incidents), reverse=True)
    return slice_terms


def reference(slices, thickness, probes, centers, batch_of, intensity):
    field = slices[:, 0] + 1j * slices[:, 1]
    padded = jnp.pad(field, ((0, 0), (HALF, HALF), (HALF, HALF)), mode="wrap")
    cosines, sines = jax.vmap(kernel_planes)(thickness)
    kernels = cosines - 1j * sines
    illuminations = probes[:, 0] + 1j * probes[:, 1]
    zero_index = jnp.int32(0)

    def per_tile(tile_index, accumulated):
        tile_row = (tile_index // N_TY).astype(jnp.int32)
        tile_col = (tile_index % N_TY).astype(jnp.int32)
        centre_table = centers[tile_row, tile_col]
        start_rows = (tile_row * TILE + centre_table[:, 0]).astype(jnp.int32)
        start_cols = (tile_col * TILE + centre_table[:, 1]).astype(jnp.int32)

        def cut_window(start_row, start_col):
            return lax.dynamic_slice(padded, (zero_index, start_row, start_col), (SLICES, WINDOW, WINDOW))

        patches = jax.vmap(cut_window)(start_rows, start_cols)
        chosen = illuminations[batch_of[tile_row, tile_col, :, 0]]
        slice_terms = jax.vmap(window_terms, in_axes=(0, 0, None, 0))(chosen, patches, kernels, intensity[tile_row, tile_col])

        def place(which, accumulated):
            start_row = start_rows[which]
            start_col = start_cols[which]
            current = lax.dynamic_slice(accumulated, (zero_index, start_row, start_col), (SLICES, WINDOW, WINDOW))
            return lax.dynamic_update_slice(accumulated, current + slice_terms[which], (zero_index, start_row, start_col))

        return lax.fori_loop(0, WIN, place, accumulated)

    accumulated = lax.fori_loop(0, N_TX * N_TY, per_tile, jnp.zeros(padded.shape, padded.dtype))
    folded_rows = accumulated[:, HALF:HALF + NX, :]
    folded_rows = folded_rows.at[:, :HALF].add(accumulated[:, HALF + NX:, :])
    folded_rows = folded_rows.at[:, NX - HALF:].add(accumulated[:, :HALF, :])
    folded = folded_rows[:, :, HALF:HALF + NY]
    folded = folded.at[:, :, :HALF].add(folded_rows[:, :, HALF + NY:])
    folded = folded.at[:, :, NY - HALF:].add(folded_rows[:, :, :HALF])
    return jnp.stack([jnp.real(folded), jnp.imag(folded)], axis=1)
```

```python
import functools
import math

import jax
import jax.numpy as jnp
import numpy as np
from jax import lax
from jax.experimental import pallas as pl
from jax.experimental.pallas import tpu as pltpu
from jax.sharding import PartitionSpec as P

F32 = jnp.float32
BF16 = jnp.bfloat16
LANES = 128
MIB = 1 << 20


VMEM = pl.BlockSpec(memory_space=pltpu.VMEM)
SMEM = pl.BlockSpec(memory_space=pltpu.SMEM)
ANY = pl.BlockSpec(memory_space=pl.ANY)


def split(x):
    hi = x.astype(BF16)
    return hi, (x - hi.astype(F32)).astype(BF16)


def dot3(lhs, rhs):
    dot = functools.partial(jnp.dot, preferred_element_type=F32)
    return dot(lhs[0], rhs[0]) + dot(lhs[1], rhs[0]) + dot(lhs[0], rhs[1])


def sandwich(waves, tables, op, conj):
    left = (tables[op, conj, 0], tables[op, conj, 1])
    right = (tables[op, 1 - conj, 0], tables[op, 1 - conj, 1])
    count = len(waves)
    size = waves[0].shape[0]
    half = dot3(split(jnp.concatenate(waves, 0)), right)
    rows = [half[i * size : (i + 1) * size] for i in range(count)]
    tall = jnp.concatenate(
        [
            jnp.concatenate([r[:, :size] for r in rows], 1),
            jnp.concatenate([r[:, size:] for r in rows], 1),
        ],
        0,
    )
    full = dot3(left, split(tall))
    return full[:size], full[size:]


def lane_index(shape):
    return lax.broadcasted_iota(jnp.int32, shape, len(shape) - 1)


def prep_kernel(slices, thick, trig, probes, tables, entering):
    size = trig.shape[-1]
    half = size // 2
    cosine, sine = trig[0], trig[1]

    def put(op, real, imag):
        plus = jnp.concatenate(
            [jnp.concatenate([real, -imag], 1), jnp.concatenate([imag, real], 1)], 0
        )
        minus = jnp.concatenate(
            [jnp.concatenate([real, imag], 1), jnp.concatenate([-imag, real], 1)], 0
        )
        for which, table in enumerate((plus, minus)):
            hi, lo = split(table)
            tables[op, which, 0] = hi
            tables[op, which, 1] = lo

    put(slices, cosine, -sine)
    row = lax.broadcasted_iota(jnp.int32, (size, size), 0)
    offset = jnp.where(row >= half, row - size, row)
    base = (offset * offset).astype(F32) * (math.pi / (half * half))
    both = jnp.concatenate([cosine, sine], 1)

    def one(s, carry):
        phase = thick[s, 0] * base
        real, imag = jnp.cos(phase), -jnp.sin(phase)
        scaled = jnp.concatenate(
            [
                jnp.concatenate([cosine * real, cosine * imag], 1),
                jnp.concatenate([sine * real, sine * imag], 1),
            ],
            0,
        )
        product = jnp.dot(
            both, scaled, preferred_element_type=F32, precision=lax.Precision.HIGHEST
        )
        put(s, product[:, :size], product[:, size:])
        return carry

    lax.fori_loop(0, slices, one, 0)
    count = probes.shape[0]
    waves = [jnp.concatenate([probes[m, 0], probes[m, 1]], 1) for m in range(count)]
    real, imag = sandwich(waves, tables, 0, 0)
    for m in range(count):
        entering[m, :, :size] = real[:, m * size : (m + 1) * size]
        entering[m, :, size:] = imag[:, m * size : (m + 1) * size]


def prep(thick_all, trig, probes):
    slices = thick_all.shape[0]
    count, _, size, _ = probes.shape
    return pl.pallas_call(
        functools.partial(prep_kernel, slices),
        out_shape=(
            jax.ShapeDtypeStruct((slices + 1, 2, 2, 2 * size, 2 * size), BF16),
            jax.ShapeDtypeStruct((count, size, 2 * size), F32),
        ),
        in_specs=[SMEM, VMEM, VMEM],
        out_specs=(VMEM, VMEM),
        compiler_params=pltpu.CompilerParams(vmem_limit_bytes=32 * MIB),
        cost_estimate=pl.CostEstimate(flops=3_000_000_000, bytes_accessed=4_000_000, transcendentals=0),
        name="prep",
    )(thick_all, trig, probes)


def pack_kernel(tile, beside, to_next, to_last):
    width = tile.shape[-1]
    strip = beside.shape[2] // 2
    tall = tile.shape[2] + 2 * strip
    part = tall // 2
    top = part - strip
    low = lane_index((part, LANES)) < LANES // 2
    for n in range(tile.shape[0]):
        for p in range(2):

            def column(start):
                upper = jnp.concatenate(
                    [beside[n, p, strip:, start : start + LANES], tile[n, p, :top, start : start + LANES]], 0
                )
                lower = jnp.concatenate(
                    [tile[n, p, top:, start : start + LANES], beside[n, p, :strip, start : start + LANES]], 0
                )
                return upper, lower

            upper, lower = column(width - LANES)
            to_next[n, p] = jnp.where(low, pltpu.roll(upper, LANES // 2, 1), lower)
            upper, lower = column(0)
            to_last[n, p] = jnp.where(low, upper, pltpu.roll(lower, LANES // 2, 1))


def ring(count, step):
    return [(i, (i + step) % count) for i in range(count)]


def rows_beside(strips):
    count = lax.axis_size("tx")
    if count == 2:
        return lax.ppermute(strips, "tx", ring(2, 1))
    half = strips.shape[-2] // 2
    return jnp.concatenate(
        [
            lax.ppermute(strips[..., :half, :], "tx", ring(count, -1)),
            lax.ppermute(strips[..., half:, :], "tx", ring(count, 1)),
        ],
        axis=-2,
    )


def columns_beside(tiles, beside):
    count, _, rows, _ = tiles.shape
    tall = rows + beside.shape[2]
    shape = jax.ShapeDtypeStruct((count, 2, tall // 2, LANES), F32)
    to_next, to_last = pl.pallas_call(
        pack_kernel,
        out_shape=(shape, shape),
        in_specs=[VMEM, VMEM],
        out_specs=(VMEM, VMEM),
        compiler_params=pltpu.CompilerParams(vmem_limit_bytes=16 * MIB),
        cost_estimate=pl.CostEstimate(flops=1_000_000, bytes_accessed=2_000_000, transcendentals=0),
        name="pack_columns",
    )(tiles, beside)
    size = lax.axis_size("ty")
    return (
        lax.ppermute(to_next, "ty", ring(size, 1)),
        lax.ppermute(to_last, "ty", ring(size, -1)),
    )


def assemble(padded, tile, beside, left, right, n):
    width = tile.shape[-1]
    planes = width // LANES
    strip = beside.shape[2] // 2
    rows = tile.shape[2]
    part = (rows + 2 * strip) // 2
    for p in range(2):
        for j in range(planes):
            where = slice(j * LANES, (j + 1) * LANES)
            padded[p, 1 + j, :strip] = beside[n, p, strip:, where]
            padded[p, 1 + j, strip : strip + rows] = tile[n, p, :, where]
            padded[p, 1 + j, strip + rows :] = beside[n, p, :strip, where]
        padded[p, 0, :part] = pltpu.roll(left[n, p], LANES // 2, 1)
        padded[p, 0, part:] = left[n, p]
        padded[p, 1 + planes, :part] = right[n, p]
        padded[p, 1 + planes, part:] = pltpu.roll(right[n, p], LANES // 2, 1)


def place_of(centers, w):
    row = centers[0, 0, w, 0]
    column = centers[0, 0, w, 1] + LANES // 2
    return row, column // LANES, lax.rem(column, LANES)


def cut_windows(padded, centers, store):
    windows = centers.shape[2]
    size = LANES

    def one(w, carry):
        row, plane, shift = place_of(centers, w)
        keep = lane_index((size, LANES)) >= shift
        for p in range(2):
            first = padded[p, plane, pl.ds(row, size), :]
            second = padded[p, plane + 1, pl.ds(row, size), :]
            store(w, p, pltpu.roll(jnp.where(keep, first, second), lax.rem(LANES - shift, LANES), 1))
        return carry

    lax.fori_loop(0, windows, one, 0)


def cut_kernel(step, fresh, centers, tile, beside, left, right, *rest):
    _, patches, padded, buffer, sems = rest if not fresh else (None, *rest)
    slices = lax.axis_size("depth")
    me = lax.axis_index("depth")
    count = tile.shape[0]
    copies = []
    for n in range(count):
        if step == 0:
            slot = me
        elif count == 2:
            slot = me - step if n == 0 else me + step
            slot = jnp.where((slot >= 0) & (slot < slices), slot, slices)
        else:
            slot = jnp.where(me >= step, me - step, jnp.where(me + step < slices, me + step, slices))
        assemble(padded, tile, beside, left, right, n)

        def store(w, p, value, n=n):
            buffer[n, w, p] = value

        cut_windows(padded, centers, store)
        copies.append(pltpu.make_async_copy(buffer.at[n], patches.at[slot], sems.at[n]))
        copies[-1].start()
    for copy in copies:
        copy.wait()


def cut(step, patches, centers, tile, beside, left, right):
    slices = lax.axis_size("depth")
    windows = centers.shape[2]
    count, _, rows, width = tile.shape
    tall = rows + beside.shape[2]
    planes = width // LANES + 2
    shape = jax.ShapeDtypeStruct((slices + 1, windows, 2, LANES, LANES), F32)
    operands = [centers, tile, beside, left, right]
    specs = [SMEM, VMEM, VMEM, VMEM, VMEM]
    if patches is not None:
        operands.append(patches)
        specs.append(ANY)
    return pl.pallas_call(
        functools.partial(cut_kernel, step, patches is None),
        out_shape=shape,
        in_specs=specs,
        out_specs=ANY,
        scratch_shapes=[
            pltpu.VMEM((2, planes, tall, LANES), F32),
            pltpu.VMEM((count, windows, 2, LANES, LANES), F32),
            pltpu.SemaphoreType.DMA((count,)),
        ],
        input_output_aliases={} if patches is None else {5: 0},
        compiler_params=pltpu.CompilerParams(vmem_limit_bytes=24 * MIB),
        cost_estimate=pl.CostEstimate(flops=2_000_000, bytes_accessed=5_000_000, transcendentals=0),
        name="cut",
    )(*operands)


def times_patch(cur, patch, w, conj):
    size = LANES
    real, imag = cur[w, :, :size], cur[w, :, size:]
    pr, pi = patch[w, 0], patch[w, 1]
    if conj:
        return jnp.concatenate([real * pr + imag * pi, imag * pr - real * pi], 1)
    return jnp.concatenate([real * pr - imag * pi, real * pi + imag * pr], 1)


def keep_waves(cur, real, imag, windows):
    size = LANES
    for w in range(windows):
        cur[w, :, :size] = real[:, w * size : (w + 1) * size]
        cur[w, :, size:] = imag[:, w * size : (w + 1) * size]


def reached(me, slices, step):
    return jnp.where(me - step <= 0, jnp.minimum(me + step + 1, slices - 1), 0)


def forward(cur, own, patches, tables, s, me, windows):
    @pl.when(s == me)
    def _():
        own[...] = cur[...]

    patch = patches.at[s]
    waves = [times_patch(cur, patch, w, False) for w in range(windows)]
    real, imag = sandwich(waves, tables, s + 1, 0)
    keep_waves(cur, real, imag, windows)


def advance_kernel(step, owners, entering, tables, patches, cur, own, held, sems):
    slices = lax.axis_size("depth")
    me = lax.axis_index("depth")
    windows = cur.shape[0]
    last = reached(me, slices, step)

    def copy(s):
        return pltpu.make_async_copy(patches.at[s], held.at[s], sems.at[s])

    def start(s, carry):
        copy(s).start()
        return carry

    lax.fori_loop(0, last, start, 0)
    for w in range(windows):
        cur[w] = entering[owners[0, 0, w, 0]]
    own[...] = jnp.zeros_like(own)

    def one(s, carry):
        copy(s).wait()
        forward(cur, own, held, tables, s, me, windows)
        return carry

    lax.fori_loop(0, last, one, 0)


def advance(step, owners, entering, tables, patches):
    slices = lax.axis_size("depth")
    windows = owners.shape[2]
    shape = jax.ShapeDtypeStruct((windows,) + entering.shape[1:], F32)
    return pl.pallas_call(
        functools.partial(advance_kernel, step),
        out_shape=(shape, shape),
        in_specs=[SMEM, VMEM, VMEM, ANY],
        out_specs=(VMEM, VMEM),
        scratch_shapes=[
            pltpu.VMEM((slices,) + patches.shape[1:], F32),
            pltpu.SemaphoreType.DMA((slices,)),
        ],
        compiler_params=pltpu.CompilerParams(vmem_limit_bytes=60 * MIB),
        cost_estimate=pl.CostEstimate(flops=8_000_000_000, bytes_accessed=9_000_000, transcendentals=0),
        name="advance",
    )(owners, entering, tables, patches)


def final_kernel(
    step,
    centers,
    tile,
    beside,
    left,
    right,
    cur_in,
    own_in,
    tables_in,
    patches,
    intensity,
    core,
    x_out,
    y_low,
    y_high,
    c_low,
    c_high,
    padded,
    held,
    cur,
    own,
    tables,
    target,
    sems,
    patch_sems,
):
    slices = lax.axis_size("depth")
    me = lax.axis_index("depth")
    windows = cur.shape[0]
    size = LANES
    final = slices - 1
    start = reached(me, slices, step)
    slot = jnp.where(me == final, 0, jnp.where(me == 0, final, slices))
    loads = [
        pltpu.make_async_copy(tables_in, tables, sems.at[0]),
        pltpu.make_async_copy(cur_in, cur, sems.at[1]),
        pltpu.make_async_copy(own_in, own, sems.at[2]),
        pltpu.make_async_copy(intensity.at[0, 0], target, sems.at[3]),
    ]
    for load in loads:
        load.start()

    def copy(s):
        return pltpu.make_async_copy(patches.at[s], held.at[s], patch_sems.at[s])

    def fetch(s, carry):
        @pl.when(s != slot)
        def _():
            copy(s).start()

        return carry

    def arrive(s, carry):
        @pl.when(s != slot)
        def _():
            copy(s).wait()

        return carry

    lax.fori_loop(0, slices, fetch, 0)
    assemble(padded, tile, beside, left, right, 0)

    def store(w, p, value):
        held[slot, w, p] = value

    cut_windows(padded, centers, store)
    for load in loads:
        load.wait()
    lax.fori_loop(0, slices, arrive, 0)

    def step_forward(s, carry):
        forward(cur, own, held, tables, s, me, windows)
        return carry

    lax.fori_loop(start, final, step_forward, 0)

    @pl.when(me == final)
    def _():
        own[...] = cur[...]

    patch = held.at[final]
    waves = [times_patch(cur, patch, w, False) for w in range(windows)]
    real, imag = sandwich(waves, tables, slices, 0)
    waves = []
    for w in range(windows):
        where = slice(w * size, (w + 1) * size)
        a, b = real[:, where], imag[:, where]
        excess = 2.0 * (a * a + b * b - target[w])
        waves.append(jnp.concatenate([excess * a, excess * b], 1))
    real, imag = sandwich(waves, tables, slices, 1)
    keep_waves(cur, real, imag, windows)

    def step_backward(i, carry):
        s = final - i
        now = held.at[s]
        back = [times_patch(cur, now, w, True) for w in range(windows)]
        back_real, back_imag = sandwich(back, tables, s, 1)
        keep_waves(cur, back_real, back_imag, windows)
        return carry

    lax.fori_loop(0, final - me, step_backward, 0)

    padded[...] = jnp.zeros_like(padded)

    def place(w, carry):
        row, plane, shift = place_of(centers, w)
        keep = lane_index((size, LANES)) >= shift
        a, b = own[w, :, :size], own[w, :, size:]
        c, d = cur[w, :, :size], cur[w, :, size:]
        for p, term in enumerate((a * c + b * d, a * d - b * c)):
            turned = pltpu.roll(term, shift, 1)
            rows = pl.ds(row, size)
            padded[p, plane, rows, :] = padded[p, plane, rows, :] + jnp.where(keep, turned, 0.0)
            padded[p, plane + 1, rows, :] = padded[p, plane + 1, rows, :] + jnp.where(keep, 0.0, turned)
        return carry

    lax.fori_loop(0, windows, place, 0)

    planes = padded.shape[1] - 2
    strip = size // 2
    tall = padded.shape[2]
    rows = tall - 2 * strip
    part = rows // 2
    low = lane_index((part, LANES)) < LANES // 2
    low_strip = lane_index((strip, LANES)) < LANES // 2
    for p in range(2):
        for j in range(planes):
            where = slice(j * LANES, (j + 1) * LANES)
            core[p, :, where] = padded[p, 1 + j, strip : strip + rows]
            x_out[0, p, :, where] = padded[p, 1 + j, :strip]
            x_out[1, p, :, where] = padded[p, 1 + j, strip + rows :]
        upper, lower = slice(strip, strip + part), slice(strip + part, strip + rows)
        above, below = slice(0, strip), slice(strip + rows, tall)
        y_low[p] = jnp.where(low, pltpu.roll(padded[p, 0, upper], LANES // 2, 1), padded[p, 0, lower])
        y_high[p] = jnp.where(low, padded[p, 1 + planes, upper], pltpu.roll(padded[p, 1 + planes, lower], LANES // 2, 1))
        c_low[p] = jnp.where(low_strip, pltpu.roll(padded[p, 0, above], LANES // 2, 1), padded[p, 0, below])
        c_high[p] = jnp.where(
            low_strip, padded[p, 1 + planes, above], pltpu.roll(padded[p, 1 + planes, below], LANES // 2, 1)
        )


def final_stage(step, centers, tile, beside, left, right, cur, own, tables, patches, intensity):
    slices = lax.axis_size("depth")
    windows = centers.shape[2]
    _, _, rows, width = tile.shape
    tall = rows + beside.shape[2]
    strip = beside.shape[2] // 2
    planes = width // LANES + 2
    shapes = [
        (2, rows, width),
        (2, 2, strip, width),
        (2, rows // 2, LANES),
        (2, rows // 2, LANES),
        (2, strip, LANES),
        (2, strip, LANES),
    ]
    return pl.pallas_call(
        functools.partial(final_kernel, step),
        out_shape=tuple(jax.ShapeDtypeStruct(s, F32) for s in shapes),
        in_specs=[SMEM, VMEM, VMEM, VMEM, VMEM, ANY, ANY, ANY, ANY, ANY],
        out_specs=(VMEM,) * len(shapes),
        scratch_shapes=[
            pltpu.VMEM((2, planes, tall, LANES), F32),
            pltpu.VMEM((slices + 1, windows, 2, LANES, LANES), F32),
            pltpu.VMEM(cur.shape, F32),
            pltpu.VMEM(own.shape, F32),
            pltpu.VMEM(tables.shape, BF16),
            pltpu.VMEM((windows, LANES, LANES), F32),
            pltpu.SemaphoreType.DMA((4,)),
            pltpu.SemaphoreType.DMA((slices,)),
        ],
        compiler_params=pltpu.CompilerParams(vmem_limit_bytes=60 * MIB),
        cost_estimate=pl.CostEstimate(flops=15_000_000_000, bytes_accessed=14_000_000, transcendentals=0),
        name="final",
    )(centers, tile, beside, left, right, cur, own, tables, patches, intensity)


def combine_kernel(core, x_in, y_next, y_last, c_next, c_last, out):
    rows, width = core.shape[1:]
    strip = x_in.shape[2]
    part = rows // 2
    low = lane_index((part, LANES)) < LANES // 2
    low_strip = lane_index((strip, LANES)) < LANES // 2
    turn = functools.partial(pltpu.roll, shift=LANES // 2, axis=1)
    first, final = slice(0, LANES), slice(width - LANES, width)
    top, bottom = slice(0, strip), slice(rows - strip, rows)
    for p in range(2):
        out[0, p] = core[p]
        out[0, p, bottom] += x_in[0, p]
        out[0, p, top] += x_in[1, p]
        out[0, p, :part, final] += jnp.where(low, 0.0, turn(y_next[p]))
        out[0, p, part:, final] += jnp.where(low, 0.0, y_next[p])
        out[0, p, :part, first] += jnp.where(low, y_last[p], 0.0)
        out[0, p, part:, first] += jnp.where(low, turn(y_last[p]), 0.0)
        out[0, p, bottom, final] += jnp.where(low_strip, 0.0, turn(c_next[p]))
        out[0, p, top, final] += jnp.where(low_strip, 0.0, c_next[p])
        out[0, p, bottom, first] += jnp.where(low_strip, c_last[p], 0.0)
        out[0, p, top, first] += jnp.where(low_strip, turn(c_last[p]), 0.0)


def fold(core, x_out, y_low, y_high, c_low, c_high):
    n_x, n_y = lax.axis_size("tx"), lax.axis_size("ty")

    def diagonal(dx, dy):
        return [
            (i * n_y + j, (i + dx) % n_x * n_y + (j + dy) % n_y) for i in range(n_x) for j in range(n_y)
        ]

    both = ("tx", "ty")
    if n_x == 2:
        x_in = lax.ppermute(x_out, "tx", ring(2, 1))
        c_next = lax.ppermute(c_low, both, diagonal(1, -1))
        c_last = lax.ppermute(c_high, both, diagonal(1, 1))
    else:
        x_in = jnp.stack(
            [lax.ppermute(x_out[0], "tx", ring(n_x, -1)), lax.ppermute(x_out[1], "tx", ring(n_x, 1))]
        )
        low = lane_index(c_low.shape) < LANES // 2
        c_next = jnp.where(
            low, lax.ppermute(c_low, both, diagonal(-1, -1)), lax.ppermute(c_low, both, diagonal(1, -1))
        )
        c_last = jnp.where(
            low, lax.ppermute(c_high, both, diagonal(-1, 1)), lax.ppermute(c_high, both, diagonal(1, 1))
        )
    y_next = lax.ppermute(y_low, "ty", ring(n_y, -1))
    y_last = lax.ppermute(y_high, "ty", ring(n_y, 1))
    return pl.pallas_call(
        combine_kernel,
        out_shape=jax.ShapeDtypeStruct((1,) + core.shape, F32),
        in_specs=[VMEM] * 6,
        out_specs=VMEM,
        compiler_params=pltpu.CompilerParams(vmem_limit_bytes=16 * MIB),
        name="combine",
    )(core, x_in, y_next, y_last, c_next, c_last)


def local(slices, thickness, probes, centers, batch_of, intensity):
    sections = lax.axis_size("depth")
    size = probes.shape[-1]
    strip = size // 2
    tile = slices
    counts = np.arange(size)
    angles = np.outer(counts, counts) % size * (2.0 * math.pi / size)
    trig = jnp.asarray(np.stack([np.cos(angles), np.sin(angles)]) / math.sqrt(size), F32)

    def strips_of(block):
        return jnp.concatenate([block[..., :strip, :], block[..., -strip:, :]], axis=-2)

    def steps(step):
        return (
            [(i, i + 1) for i in range(step - 1, sections - 1)],
            [(i, i - 1) for i in range(1, sections - step + 1)],
        )

    right_pairs, left_pairs = steps(1)
    rising = lax.ppermute(tile, "depth", right_pairs)
    falling = lax.ppermute(tile, "depth", left_pairs)
    spread = jnp.broadcast_to(thickness.reshape(1, 1), (sections, 1))
    all_thick = lax.all_to_all(spread, "depth", split_axis=0, concat_axis=0, tiled=True)
    beside = rows_beside(strips_of(tile))
    left, right = columns_beside(tile, beside)
    tables, entering = prep(all_thick, trig, probes)
    patches = cut(0, None, centers, tile, beside, left, right)
    only = None
    for step in range(1, sections):
        if step > 1:
            right_pairs, left_pairs = steps(step)
            if only is not None and 2 * step > sections + 1:
                only = lax.ppermute(only, "depth", right_pairs + left_pairs)
            else:
                rising = lax.ppermute(rising, "depth", right_pairs)
                falling = lax.ppermute(falling, "depth", left_pairs)
        if 2 * step >= sections:
            if only is None or 2 * step <= sections + 1:
                only = rising + falling
            now = only
        else:
            now = jnp.concatenate([rising, falling], axis=0)
        beside = rows_beside(strips_of(now))
        left, right = columns_beside(now, beside)
        if step < sections - 1:
            patches = cut(step, patches, centers, now, beside, left, right)
    cur, own = advance(sections - 2, batch_of, entering, tables, patches)
    parts = final_stage(
        sections - 2, centers, now, beside, left, right, cur, own, tables, patches, intensity
    )
    return fold(*parts)


def solution(mesh):
    placed = (
        P("depth", None, "tx", "ty"),
        P("depth"),
        P(),
        P("tx", "ty", None, None),
        P("tx", "ty", None, None),
        P("tx", "ty", None, None, None),
    )
    return jax.shard_map(
        local, mesh=mesh, in_specs=placed, out_specs=P("depth", None, "tx", "ty"), check_vma=False
    )
```
